128 devices in a mesh: grp: 2 (over y_lo), fsdp: 64 (over y_hi, z, x, core).
Axes of the slice: x: 4, y: 4 (y_hi: 2, y_lo: 2; y = y_hi * 2 + y_lo), z: 4, core: 2. Of those that a mesh axis runs over, the one named last changes fastest.
Arguments:
- hidden: bfloat16 [2, 49152, 4096], P('grp', 'fsdp'), may hold values from -400 to 400
- weights: bfloat16 [2, 1024, 4096], P('grp', 'fsdp'), may hold values from -6 to 6
- gain: float32 [2, 4096], P('grp'), may hold values from 0.1 to 1.9
- cotangent: bfloat16 [49152, 1024], P('fsdp'), may hold values from -16 to 16
- send_row: int32 [2, 4096], P('grp', 'fsdp'), may hold values from 0 to 5
- send_owner: int32 [2, 4096, 1], P('grp', 'fsdp'), may hold values from 0 to 63, as said below
- send_target: int32 [2, 4096], P('grp', 'fsdp'), may hold values from 0 to 5
Outputs:
- encoded: bfloat16 [2, 49152, 1024], P('grp', 'fsdp')
- new_weights: bfloat16 [2, 1024, 4096], P('grp', 'fsdp')
- delivered: float32 [2, 384, 1024], P('grp', 'fsdp')
The draws below stay inside these ranges and needn't reach their ends.
Inputs may be any that keep to these rules, and one draw needn't show every extreme that they name: `send_owner`: among the 64 entries of one device no owner is named more than 4 times; every device names some owner exactly 4 times.
All inputs are finite; a program needn't handle non-finite values.
Results may differ from the reference program's by a relative error of at most 0.005.
Values may be sent and summed in bfloat16 or wider, within the bound.
A program may use at most 128 MiB of HBM per device.

```python
import jax
import jax.numpy as jnp
import numpy as np
from jax import lax

D = 4096
KV = 1024
SEG = 128
NSEND = 64
CAP = 4
POOL_DEV = 6
TOK = 49152
N_FSDP = 64


def draw_hidden(key, part):
    keys = jax.random.split(jax.random.fold_in(key, 11), 3)
    base = jax.random.normal(keys[0], (2, TOK, D), jnp.float32)
    base = jnp.clip(base, -4.0, 4.0)
    row_scale = jnp.exp(jax.random.uniform(keys[1], (2, TOK, 1), jnp.float32, 0.0, 2.3))
    col_scale = jnp.exp(jax.random.uniform(keys[2], (1, 1, D), jnp.float32, 0.0, 2.3))
    return (base * row_scale * col_scale).astype(jnp.bfloat16)


def draw_send_owner(key, part):
    devices = N_FSDP
    others = np.array([o for o in range(devices) if o not in (1, devices - 1, devices // 2)], dtype=np.int32)
    base_table = jnp.asarray(np.array([1, devices - 1, devices // 2], dtype=np.int32))
    remain = NSEND - CAP - 2
    cycle = jnp.arange(remain, dtype=jnp.int32) % others.shape[0]
    others_table = jnp.asarray(others)
    device_ids = jnp.arange(devices, dtype=jnp.int32)

    def one_device(sub_key, device):
        pick_key, order_key = jax.random.split(sub_key)
        heavy = jax.random.randint(pick_key, (), 0, 3, dtype=jnp.int32)
        heavy_offset = base_table[heavy]
        light_one = base_table[(heavy + 1) % 3]
        light_two = base_table[(heavy + 2) % 3]
        fixed_part = jnp.concatenate([jnp.full((CAP,), heavy_offset, jnp.int32), jnp.stack([light_one, light_two]).astype(jnp.int32)])
        order = jax.random.permutation(order_key, others.shape[0])
        offsets = jnp.concatenate([fixed_part, others_table[order][cycle]])
        return ((device + offsets) % devices).astype(jnp.int32)
    groups = []
    for group in range(2):
        keys = jax.random.split(jax.random.fold_in(key, 31 + group), devices)
        owners = jax.vmap(one_device)(keys, device_ids)
        groups.append(owners.reshape(devices * NSEND, 1))
    return jnp.stack(groups).astype(jnp.int32)


def set_ends(result, stream_key, smallest, largest):
    spot = [jax.random.randint(jax.random.fold_in(stream_key, axis), (), 0, length) for axis, length in enumerate(result.shape)]
    longest = result.shape.index(max(result.shape))
    neighbour = spot[:longest] + [(spot[longest] + 1) % result.shape[longest]] + spot[longest + 1:]
    return result.at[tuple(spot)].set(smallest).at[tuple(neighbour)].set(largest)


def with_spikes(entries, stream_key, source, target, shards_of, factor):
    owner, partner = [(jnp.arange(entries.shape[dim]) // (entries.shape[dim] // shards_of)).reshape([-1 if axis == dim else 1 for axis in range(entries.ndim)]) for dim in (source, target)]
    chosen = jax.random.permutation(stream_key, shards_of)[partner]
    strong = (owner == chosen) | (owner == (partner + shards_of // 2) % shards_of)
    return jnp.where(strong, factor * entries, entries)


def level_of(key, shape, shards, smallest, largest):
    factor_of, own = 1.0, jax.random.fold_in(key, 6)
    for dim, parts in shards:
        draws = jnp.exp(jax.random.uniform(jax.random.fold_in(own, dim), (parts,), jnp.float32, smallest / len(shards), largest / len(shards)))
        factor_of = factor_of * jnp.repeat(draws, shape[dim] // parts).reshape([-1 if axis == dim else 1 for axis in range(len(shape))])
    return factor_of


def centred(own_key, dims, width, most, shards=(), kind=jnp.bfloat16):
    drawn = width * jax.random.normal(own_key, dims, jnp.float32)
    if shards:
        drawn = drawn * level_of(own_key, dims, shards, -0.22, 0.18)
    return jnp.clip(drawn, -most, most).astype(kind)


def noise_with(own_key, extent, width, limit, cuts, heavy, kind=jnp.bfloat16):
    drawn = width * jax.random.normal(own_key, extent, jnp.float32)
    if cuts:
        drawn = drawn * level_of(own_key, extent, cuts, -0.22, 0.18)
    return jnp.clip(with_spikes(drawn, jax.random.fold_in(own_key, 3), *heavy), -limit, limit).astype(kind)


def setup_inputs(seed: int = 0) -> dict:
    key_of = jax.random.split(jax.random.key(seed), 8)
    return {
        "hidden": draw_hidden(jax.random.fold_in(key_of[7], 71), 0),
        "weights": centred(key_of[1], (2, KV, D), 1.0, 6.0, ((0, 2), (1, 64))),
        "gain": jnp.clip(1.0 + 0.18 * jax.random.normal(key_of[2], (2, D), jnp.float32), 0.1, 1.9),
        "cotangent": noise_with(key_of[3], (TOK, KV), 1.0, 16.0, ((0, 64),), (0, 1, 64, 4.0)),
        "send_row": set_ends(jax.random.randint(key_of[4], (2, N_FSDP * NSEND), 0, POOL_DEV), jax.random.fold_in(key_of[4], 1), 0, POOL_DEV - 1).astype(jnp.int32),
        "send_owner": draw_send_owner(jax.random.fold_in(key_of[7], 71), 0),
        "send_target": set_ends(jax.random.randint(key_of[6], (2, N_FSDP * NSEND), 0, POOL_DEV), jax.random.fold_in(key_of[6], 1), 0, POOL_DEV - 1).astype(jnp.int32),
    }


epsilon = 1e-06
learn_rate = 0.25
momentum = 0.75

def normalize(states, scale_gain):
    values = states.astype(jnp.float32)
    mean_square = lax.optimization_barrier(jnp.mean(values * values, axis=-1, keepdims=True))
    return (values * lax.rsqrt(mean_square + epsilon) * scale_gain).astype(jnp.bfloat16)

def reference(hidden, weights, gain, cotangent, send_row, send_owner, send_target):
    factor = D ** (-0.5)
    encoded_list = []
    pooled_list = []
    normed_list = []
    for group in range(2):
        normed = normalize(hidden[group], gain[group])
        normed_list.append(normed)
        values = jnp.dot(normed, weights[group].T, preferred_element_type=jnp.float32) * factor
        encoded_list.append(values.astype(jnp.bfloat16))
        pooled = lax.optimization_barrier(jnp.mean(values.reshape(TOK // SEG, SEG, KV), axis=1)).astype(jnp.bfloat16)
        pooled_list.append(pooled)
    grad = jnp.dot(cotangent.T, normed_list[0], preferred_element_type=jnp.float32) * factor
    scale_row = jnp.sqrt(lax.optimization_barrier(jnp.mean(grad * grad, axis=1, keepdims=True)) + epsilon)
    trained = (weights[0].astype(jnp.float32) - learn_rate * grad / scale_row).astype(jnp.bfloat16)
    averaged = (momentum * weights[1].astype(jnp.float32) + (1.0 - momentum) * trained.astype(jnp.float32)).astype(jnp.bfloat16)
    new_weights = jnp.stack([trained, averaged])
    device_of = (jnp.arange(N_FSDP * NSEND, dtype=jnp.int32) // NSEND).astype(jnp.int32)
    delivered_list = []
    for target_group in range(2):
        source_group = 1 - target_group
        picked = (device_of * POOL_DEV + send_row[source_group]).astype(jnp.int32)
        rows = pooled_list[source_group][picked].astype(jnp.float32)
        places = (send_owner[source_group, :, 0] * POOL_DEV + send_target[source_group]).astype(jnp.int32)
        delivered_list.append(jax.ops.segment_sum(rows, places, num_segments=N_FSDP * POOL_DEV))
    return (jnp.stack(encoded_list), new_weights, jnp.stack(delivered_list))
```

```python
import jax
import jax.numpy as jnp
from jax import lax
from jax.experimental import pallas as pl
from jax.experimental.pallas import tpu as pltpu
from jax.sharding import PartitionSpec as P

MESH = pl.DeviceIdType.MESH
BF = jnp.bfloat16
F32 = jnp.float32

SEG = 128
TOKD = 768
D = 4096
KV = 1024
ROWS = 16
POOL = 6
NC = 4
CW = D // NC
NV = 4
VW = KV // NV
EPS = 1e-06
LEARN = 0.25
MOMENTUM = 0.75


def kernel(
    hid, wgt, gain, cot, srow, sown, stgt,
    enc, neww, deliv,
    N, CT, CO, W, G, PR, QA, QB, QY, FG, TR, RT, WN, E, PO, MS, MR,
    s_in, s_y, s_sh, s_sb, s_sa, s_ps, s_pr,
    r_ps, r_pr, r_as, r_ar, r_bs, r_br, r_ys, r_yr,
    t_s, t_r, m1s, m1r, m2s, m2r, m3s, m3r, s_out,
):
    g = lax.axis_index("grp")
    f = lax.axis_index("fsdp")
    c = lax.rem(f, 2)
    x = lax.rem(lax.div(f, 2), 4)
    z = lax.rem(lax.div(f, 8), 4)
    yh = lax.div(f, 32)
    pa = z + c * (x - z)
    pb = x + c * (z - x)
    m, o = yh, 1 - yh

    def up(p, by):
        return lax.rem(p + by, 4)

    def dev(gg, yy, a, b, cc):
        zz = a + c * (b - a)
        xx = b + c * (a - b)
        return (gg, ((yy * 4 + zz) * 4 + xx) * 2 + cc)

    a1, a2, a3 = up(pa, 1), up(pa, 2), up(pa, 3)
    b1, b2, b3 = up(pb, 1), up(pb, 2), up(pb, 3)
    A_R, A_L, A_O = dev(g, yh, a1, pb, c), dev(g, yh, a3, pb, c), dev(g, yh, a2, pb, c)
    B_R, B_L = dev(g, yh, pa, b1, c), dev(g, yh, pa, b3, c)
    Y_O = dev(g, o, pa, pb, c)
    CORE = dev(g, yh, pa, pb, 1 - c)
    CROSS = [dev(1 - g, yy, pa, bb, c) for yy in range(2) for bb in range(4)]
    OTHER = dev(1 - g, yh, pa, pb, c)

    barrier = pltpu.get_barrier_semaphore()
    peers = [A_R, A_L, A_O, B_R, B_L, Y_O, CORE] + CROSS
    for peer in peers:
        pl.semaphore_signal(barrier, inc=1, device_id=peer, device_id_type=MESH)

    def rc(src, dst, ss, rs, to):
        return pltpu.make_async_remote_copy(
            src_ref=src, dst_ref=dst, send_sem=ss, recv_sem=rs, device_id=to, device_id_type=MESH
        )

    pending = []
    pending0 = []

    def send(make, only0=False):
        make().start()
        (pending0 if only0 else pending).append(make)

    own = W.at[c, yh, pa, pb]
    w_in = pltpu.make_async_copy(wgt.at[0], own, s_in.at[0])
    w_in.start()
    NH = 6
    HR = TOKD // NH
    loads = []
    for i in range(NH):
        cp = pltpu.make_async_copy(
            hid.at[0, pl.ds(i * HR, HR)], N.at[pl.ds(i * HR, HR)], s_in.at[1 + i]
        )
        cp.start()
        loads.append(cp)
    c_in = pltpu.make_async_copy(cot, CO, s_in.at[1 + NH])
    c_in.start()

    def norm(i):
        loads[i].wait()

        def body(j, carry):
            rows = pl.ds(pl.multiple_of(i * HR + j * 16, 16), 16)
            v = N[rows, :].astype(F32)
            ms = jnp.mean(v * v, axis=1, keepdims=True)
            N[rows, :] = (v * lax.rsqrt(ms + EPS) * gain[...]).astype(BF)
            return carry

        lax.fori_loop(0, HR // 16, body, 0)

    def shard(yy, a, b):
        return W.at[c, yy, a, b]

    def sh_idx(yy, a, b):
        return (yy * 4 + a) * 4 + b

    def sh_send(yy, a, b, to, sem):
        def make():
            return rc(shard(yy, a, b), shard(yy, a, b), sem, s_sh.at[sh_idx(yy, a, b)], to)

        send(make)

    def sh_wait(yy, a, b):
        rc(shard(yy, a, b), shard(yy, a, b), s_y.at[0], s_sh.at[sh_idx(yy, a, b)], A_R).wait_recv()

    bsem = iter(range(6))
    asem = iter(range(24))

    def b_send(yy, b, to):
        sh_send(yy, pa, b, to, s_sb.at[next(bsem)])

    def a_send(yy, a, b, to):
        sh_send(yy, a, b, to, s_sa.at[next(asem)])

    def a_both(yy, b):
        a_send(yy, pa, b, A_R)
        a_send(yy, pa, b, A_L)

    def a_relay(yy, b, right):
        sh_wait(yy, a3, b)
        sh_wait(yy, a1, b)
        if right:
            a_send(yy, a3, b, A_R)
        else:
            a_send(yy, a1, b, A_L)

    psem = iter(range(8))

    def core_send(yy, a):
        i = next(psem)

        def make():
            return rc(W.at[c, yy, a], W.at[c, yy, a], s_ps.at[i], s_pr.at[yy * 4 + a], CORE)

        send(make)

    def core_wait(yy, a):
        rc(W.at[1 - c, yy, a], W.at[1 - c, yy, a], s_ps.at[0], s_pr.at[yy * 4 + a], CORE).wait_recv()

    def ag0():
        w_in.wait()
        sh_send(m, pa, pb, Y_O, s_y.at[0])
        b_send(m, pb, B_R)
        b_send(m, pb, B_L)
        a_both(m, pb)

    def ag1():
        sh_wait(m, pa, b3)
        sh_wait(m, pa, b1)
        b_send(m, b3, B_R)
        sh_wait(o, pa, pb)
        b_send(o, pb, B_R)
        b_send(o, pb, B_L)
        a_both(m, b3)
        a_both(m, b1)
        a_both(o, pb)

    def ag2():
        a_relay(m, pb, True)
        sh_wait(o, pa, b3)
        sh_wait(o, pa, b1)
        b_send(o, b1, B_L)
        sh_wait(m, pa, b2)
        a_both(m, b2)
        core_send(m, pa)
        a_both(o, b3)
        a_both(o, b1)

    def ag3():
        a_relay(m, b3, True)
        a_relay(m, b1, False)
        a_relay(o, pb, False)
        sh_wait(o, pa, b2)
        a_both(o, b2)
        core_send(o, pa)

    def ag4():
        a_relay(m, b2, False)
        core_send(m, a3)
        core_send(m, a1)
        a_relay(o, b3, False)
        a_relay(o, b1, True)
        a_relay(o, b2, True)
        core_send(o, a3)
        core_send(o, a1)

    def ag5():
        for yy in (m, o):
            for b in (pb, b3, b1, b2):
                sh_wait(yy, a2, b)
            core_send(yy, a2)

    def ag6():
        for yy in range(2):
            for a in range(4):
                core_wait(yy, a)

    def only0(fn):
        pl.when(g == 0)(fn)

    def cols(k):
        return pl.ds(k * CW, CW)

    def turn():
        c_in.wait()

        def body(i, carry):
            at = pl.ds(pl.multiple_of(i * 128, 128), 128)
            CT[at, :] = CO[:, at].T
            return carry

        lax.fori_loop(0, KV // 128, body, 0)

    def s0(k):
        @pl.loop(0, CW // 256)
        def _(j):
            at = pl.ds(pl.multiple_of(k * CW + j * 256, 256), 256)
            for yy in range(2):
                part = jnp.dot(
                    CT[pl.ds(yy * 512, 512), :], N[:, at], preferred_element_type=F32
                ).astype(BF)
                for zz in range(4):
                    for xx in range(4):
                        for cc in range(2):
                            r = ((zz * 4 + xx) * 2 + cc) * 16
                            aa, bb = (zz, xx) if cc == 0 else (xx, zz)
                            G[cc, yy, aa, bb, :, at] = part[r : r + 16, :]

        send(
            lambda: rc(G.at[1 - c, :, :, :, :, cols(k)], PR.at[k], r_ps.at[k], r_pr.at[k], CORE),
            True,
        )

    def recv(buf, sem):
        rc(buf, buf, r_ps.at[0], sem, CORE).wait_recv()

    def s1(k):
        recv(PR.at[k], r_pr.at[k])

        @pl.loop(0, 32)
        def _(i):
            yy, a, b = i // 16, (i // 4) % 4, i % 4
            G[c, yy, a, b, :, cols(k)] = (
                G[c, yy, a, b, :, cols(k)].astype(F32) + PR[k, yy, a, b].astype(F32)
            ).astype(BF)

        def part(yy, a):
            return G.at[c, yy, a, :, :, cols(k)]

        for q, yy, a, to in ((0, 0, a2, A_R), (1, 1, a2, A_L), (2, 1, a1, A_R), (3, 0, a3, A_L)):
            send(
                lambda q=q, yy=yy, a=a, to=to: rc(
                    part(yy, a), QA.at[k, q], r_as.at[k, q], r_ar.at[k, q], to
                ),
                True,
            )

    def s2(k):
        for q, yy, a, to in ((0, 0, a1, A_R), (1, 1, a3, A_L)):
            recv(QA.at[k, q], r_ar.at[k, q])

            @pl.loop(0, 4)
            def _(b, q=q, yy=yy, a=a):
                G[c, yy, a, b, :, cols(k)] = (
                    G[c, yy, a, b, :, cols(k)].astype(F32) + QA[k, q, b].astype(F32)
                ).astype(BF)

            send(
                lambda q=q, yy=yy, a=a, to=to: rc(
                    G.at[c, yy, a, :, :, cols(k)], QA.at[k, 4 + q],
                    r_as.at[k, 4 + q], r_ar.at[k, 4 + q], to,
                ),
                True,
            )

    def s3(k):
        for q in (2, 3, 4, 5):
            recv(QA.at[k, q], r_ar.at[k, q])
        for yy, q0, q1 in ((0, 3, 4), (1, 2, 5)):

            @pl.loop(0, 4)
            def _(b, yy=yy, q0=q0, q1=q1):
                G[c, yy, pa, b, :, cols(k)] = (
                    G[c, yy, pa, b, :, cols(k)].astype(F32)
                    + (QA[k, q0, b].astype(F32) + QA[k, q1, b].astype(F32))
                ).astype(BF)

        for q, yy, b, to in ((0, 0, b2, B_R), (1, 1, b2, B_L), (2, 1, b1, B_R), (3, 0, b3, B_L)):
            send(
                lambda q=q, yy=yy, b=b, to=to: rc(
                    G.at[c, yy, pa, b, :, cols(k)], QB.at[k, q], r_bs.at[k, q], r_br.at[k, q], to
                ),
                True,
            )

    def s4(k):
        for q, yy, b, to in ((0, 0, b1, B_R), (1, 1, b3, B_L)):
            recv(QB.at[k, q], r_br.at[k, q])
            G[c, yy, pa, b, :, cols(k)] = (
                G[c, yy, pa, b, :, cols(k)].astype(F32) + QB[k, q].astype(F32)
            ).astype(BF)
            send(
                lambda q=q, yy=yy, b=b, to=to: rc(
                    G.at[c, yy, pa, b, :, cols(k)], QB.at[k, 4 + q],
                    r_bs.at[k, 4 + q], r_br.at[k, 4 + q], to,
                ),
                True,
            )

    def s5(k):
        for q in (2, 3, 4, 5):
            recv(QB.at[k, q], r_br.at[k, q])
        for yy, q0, q1 in ((0, 3, 4), (1, 2, 5)):
            G[c, yy, pa, pb, :, cols(k)] = (
                G[c, yy, pa, pb, :, cols(k)].astype(F32)
                + (QB[k, q0].astype(F32) + QB[k, q1].astype(F32))
            ).astype(BF)
        send(
            lambda: rc(G.at[c, o, pa, pb, :, cols(k)], QY.at[k], r_ys.at[k], r_yr.at[k], Y_O), True
        )

    def s6(k):
        recv(QY.at[k], r_yr.at[k])
        FG[:, cols(k)] = (
            G[c, yh, pa, pb, :, cols(k)].astype(F32) + QY[k].astype(F32)
        ) * (D ** -0.5)

    outs = []

    def values(n):
        yy, z0 = n // 2, (n % 2) * 2
        for i in range(2):
            for xx in range(4):
                r = i * 128 + xx * 32
                WN[pl.ds(r, 16), :] = W[0, yy, z0 + i, xx]
                WN[pl.ds(r + 16, 16), :] = W[1, yy, xx, z0 + i]

        @pl.loop(0, 2)
        def _(h):
            rows = pl.ds(pl.multiple_of(h * 384, 128), 384)
            v = lax.dot_general(
                N[rows, :], WN[...], (((1,), (1,)), ((), ())), preferred_element_type=F32
            ) * (D ** -0.5)
            E[rows, pl.ds(n * VW, VW)] = v.astype(BF)
            p = jnp.mean(v.reshape(3, SEG, VW), axis=1)
            PO[h, 0:3, pl.ds(n * VW, VW)] = p

        cp = pltpu.make_async_copy(
            E.at[:, pl.ds(n * VW, VW)], enc.at[0, :, pl.ds(n * VW, VW)], s_out.at[n]
        )
        cp.start()
        outs.append(cp)

    def msg1():
        p = jnp.concatenate([PO[0, 0:3, :], PO[1, 0:3, :], jnp.zeros((2, KV), F32)], axis=0)
        lo, hi = p[:, 0:512], p[:, 512:1024]
        pad = jnp.zeros((1, 64), F32)
        label = jnp.concatenate(
            [
                srow[...].astype(F32), pad, sown[...].astype(F32), pad,
                stgt[...].astype(F32), pad, jnp.zeros((1, 128), F32),
            ],
            axis=1,
        )
        line = lax.broadcasted_iota(jnp.int32, (8, 512), 0)
        lo = jnp.where(line == 6, jnp.broadcast_to(label, (8, 512)), lo)
        MS[...] = jnp.concatenate([lo, hi], axis=0).astype(BF)
        for i in range(8):
            send(
                lambda i=i: rc(
                    MS, MR.at[c, yh, pa, pb], m1s.at[i], m1r.at[yh * 4 + pb], CROSS[i]
                )
            )

    def msg2():
        for yy in range(2):
            for b in range(4):
                rc(MS, MR.at[c, yy, pa, b], m1s.at[0], m1r.at[yy * 4 + b], Y_O).wait_recv()
        for i, to in enumerate((A_R, A_L, A_O)):
            send(
                lambda i=i, to=to: rc(
                    MR.at[c, :, pa], MR.at[c, :, pa], m2s.at[i], m2r.at[pa], to
                )
            )

    def msg3():
        for a in (a1, a3, a2):
            rc(MR.at[c, :, a], MR.at[c, :, a], m2s.at[0], m2r.at[a], A_R).wait_recv()
        send(lambda: rc(MR.at[c], MR.at[c], m3s, m3r, CORE))

    def deliver():
        rc(MR.at[1 - c], MR.at[1 - c], m3s, m3r, CORE).wait_recv()
        rows = MR[...].reshape(64, 16, 512)
        lab = rows[:, :, 0:384].astype(F32)[:, 6:7, :]
        mine = f.astype(F32)
        line = lax.broadcasted_iota(jnp.int32, (64, 16, 64), 1)
        line = jnp.where(line >= 8, line - 8, line).astype(F32)
        code = jnp.where(lab[:, :, 128:192] == mine, lab[:, :, 0:64] * 8 + lab[:, :, 256:320], -1.0)
        code = jnp.broadcast_to(code, (64, 16, 64)) - line * 8
        counts = [
            jnp.sum(jnp.where(code == t, 1.0, 0.0), axis=2, keepdims=True) for t in range(POOL)
        ]
        upper = lax.broadcasted_iota(jnp.int32, (64, 16, 1), 1) < 8
        none = jnp.zeros((64, 16, 2), F32)
        table = jnp.concatenate(
            [jnp.where(upper, n, 0.0) for n in counts] + [none]
            + [jnp.where(upper, 0.0, n) for n in counts] + [none],
            axis=2,
        ).reshape(1024, 16)
        out = lax.dot_general(
            table.astype(BF), rows.reshape(1024, 512), (((0,), (0,)), ((), ())),
            preferred_element_type=F32,
        )
        deliv[0, :, 0:512] = out[0:POOL, :]
        deliv[0, :, 512:1024] = out[8 : 8 + POOL, :]

    def update0():
        gr = FG[...]
        scale = jnp.sqrt(jnp.mean(gr * gr, axis=1, keepdims=True) + EPS)
        t = (W[c, yh, pa, pb].astype(F32) - LEARN * gr / scale).astype(BF)
        TR[...] = t
        neww[0] = t
        send(lambda: rc(TR, RT, t_s, t_r, OTHER), True)

    def update1():
        rc(TR, RT, t_s, t_r, OTHER).wait_recv()
        neww[0] = (
            MOMENTUM * W[c, yh, pa, pb].astype(F32) + (1.0 - MOMENTUM) * RT[...].astype(F32)
        ).astype(BF)

    norm(0)
    norm(1)
    pl.semaphore_wait(barrier, len(peers))
    ag0()
    for i in range(2, NH):
        norm(i)
    only0(turn)
    only0(lambda: s0(0))
    ag1()

    @only0
    def _():
        s0(1)
        s1(0)

    ag2()

    @only0
    def _():
        s0(2)
        s1(1)
        s2(0)

    ag3()

    @only0
    def _():
        s0(3)
        s1(2)
        s2(1)
        s3(0)

    ag4()

    @only0
    def _():
        s1(3)
        s2(2)
        s3(1)
        s4(0)

    ag5()

    @only0
    def _():
        s2(3)
        s3(2)
        s4(1)
        s5(0)

    ag6()
    values(0)

    @only0
    def _():
        s3(3)
        s4(2)
        s5(1)
        s6(0)

    values(1)

    @only0
    def _():
        s4(3)
        s5(2)
        s6(1)

    values(2)

    @only0
    def _():
        s5(3)
        s6(2)

    values(3)
    msg1()

    @only0
    def _():
        s6(3)
        update0()

    msg2()
    msg3()
    deliver()
    pl.when(g == 1)(update1)
    c_in_wait = pl.when(g == 1)
    c_in_wait(lambda: c_in.wait())
    for cp in outs:
        cp.wait()
    for make in pending:
        make().wait_send()

    @only0
    def _():
        for make in pending0:
            make().wait_send()


def on_device(hidden, weights, gain, cotangent, send_row, send_owner, send_target):
    dma = pltpu.SemaphoreType.DMA
    vm = pltpu.VMEM
    anywhere = pl.BlockSpec(memory_space=pl.ANY)
    vmem = pl.BlockSpec(memory_space=pltpu.VMEM)
    return pl.pallas_call(
        kernel,
        out_shape=(
            jax.ShapeDtypeStruct((1, TOKD, KV), BF),
            jax.ShapeDtypeStruct((1, ROWS, D), BF),
            jax.ShapeDtypeStruct((1, POOL, KV), F32),
        ),
        in_specs=[anywhere, anywhere, vmem, anywhere, vmem, vmem, vmem],
        out_specs=(anywhere, vmem, vmem),
        scratch_shapes=[
            vm((TOKD, D), BF),
            vm((KV, TOKD), BF),
            vm((TOKD, KV), BF),
            vm((2, 2, 4, 4, ROWS, D), BF),
            vm((2, 2, 4, 4, ROWS, D), BF),
            vm((NC, 2, 4, 4, ROWS, CW), BF),
            vm((NC, 6, 4, ROWS, CW), BF),
            vm((NC, 6, ROWS, CW), BF),
            vm((NC, ROWS, CW), BF),
            vm((ROWS, D), F32),
            vm((ROWS, D), BF),
            vm((ROWS, D), BF),
            vm((VW, D), BF),
            vm((TOKD, KV), BF),
            vm((2, 8, KV), F32),
            vm((16, 512), BF),
            vm((2, 2, 4, 4, 16, 512), BF),
            dma((8,)),
            dma((1,)),
            dma((32,)),
            dma((6,)),
            dma((24,)),
            dma((8,)),
            dma((8,)),
            dma((NC,)),
            dma((NC,)),
            dma((NC, 6)),
            dma((NC, 6)),
            dma((NC, 6)),
            dma((NC, 6)),
            dma((NC,)),
            dma((NC,)),
            dma,
            dma,
            dma((8,)),
            dma((8,)),
            dma((3,)),
            dma((4,)),
            dma,
            dma,
            dma((NV,)),
        ],
        compiler_params=pltpu.CompilerParams(
            collective_id=0, has_side_effects=True, vmem_limit_bytes=64 * 1024 * 1024 - 131072
        ),
    )(
        hidden, weights, gain, cotangent, send_row, send_owner.reshape(1, -1), send_target
    )


def solution(mesh):
    in_specs = (
        P("grp", "fsdp", None),
        P("grp", "fsdp", None),
        P("grp", None),
        P("fsdp", None),
        P("grp", "fsdp"),
        P("grp", "fsdp", None),
        P("grp", "fsdp"),
    )
    out_specs = (P("grp", "fsdp", None), P("grp", "fsdp", None), P("grp", "fsdp", None))
    return jax.shard_map(
        on_device, mesh=mesh, in_specs=in_specs, out_specs=out_specs, check_vma=False
    )
```

```python
import jax
import jax.numpy as jnp
from jax import lax
from jax.experimental import pallas as pl
from jax.experimental.pallas import tpu as pltpu
from jax.sharding import PartitionSpec as P

MESH = pl.DeviceIdType.MESH
BF = jnp.bfloat16
F32 = jnp.float32

SEG = 128
TOKD = 768
D = 4096
KV = 1024
ROWS = 16
POOL = 6
NC = 4
CW = D // NC
NV = 4
LENT = (0,)
VW = KV // NV
EPS = 1e-06
LEARN = 0.25
MOMENTUM = 0.75


def kernel(
    hid, wgt, gain, cot, srow, sown, stgt,
    enc, neww, deliv,
    N, CT, CO, W, G, PR, QA, QB, FG, TR, RT, WN, E, PO, MS, MR, SP, DP,
    s_in, ag_s, ag_b, ag_a, ag_r, rs_s, rs_r, x_r, t_s, t_r, ms_s, ms_r, s_out,
):
    g = lax.axis_index("grp")
    f = lax.axis_index("fsdp")
    c = lax.rem(f, 2)
    x = lax.rem(lax.div(f, 2), 4)
    z = lax.rem(lax.div(f, 8), 4)
    yh = lax.div(f, 32)
    pa = z + c * (x - z)
    pb = x + c * (z - x)
    m, o = yh, 1 - yh

    def up(p, by):
        return lax.rem(p + by, 4)

    def dev(gg, yy, a, b, cc):
        zz = a + c * (b - a)
        xx = b + c * (a - b)
        return (gg, ((yy * 4 + zz) * 4 + xx) * 2 + cc)

    a1, a2, a3 = up(pa, 1), up(pa, 2), up(pa, 3)
    b1, b2, b3 = up(pb, 1), up(pb, 2), up(pb, 3)
    A_R, A_L, A_O = dev(g, yh, a1, pb, c), dev(g, yh, a3, pb, c), dev(g, yh, a2, pb, c)
    B_R, B_L = dev(g, yh, pa, b1, c), dev(g, yh, pa, b3, c)
    Y_O = dev(g, o, pa, pb, c)
    CORE = dev(g, yh, pa, pb, 1 - c)
    TEAM = [dev(g, yh, pa, b, c) for b in (b1, b3, b2)] + [
        dev(g, o, pa, b, c) for b in (b1, b3, b2, pb)
    ]
    CROSS = [dev(1 - g, yy, pa, bb, c) for yy in range(2) for bb in range(4)]
    OTHER = dev(1 - g, yh, pa, pb, c)
    LEND = dev(1 - g, yh + c * (1 - 2 * yh), pa, pb, c)

    barrier = pltpu.get_barrier_semaphore()
    flip = 1 - 2 * c
    AIM = [f] + [dev(g, yh, a, pb, c)[1] for a in (a1, a3, a2)]
    AIM = AIM + [i + flip for i in AIM]
    NEAR = [(g, dev(g, yh, pa, b, c)[1] + flip) for b in (b1, b3, b2)]
    peers = [(g, i) for i in AIM[1:]] + NEAR + TEAM + CROSS
    for peer in peers:
        pl.semaphore_signal(barrier, inc=1, device_id=peer, device_id_type=MESH)

    def rc(src, dst, ss, rs, to):
        return pltpu.make_async_remote_copy(
            src_ref=src, dst_ref=dst, send_sem=ss, recv_sem=rs, device_id=to, device_id_type=MESH
        )

    def recv(buf, sem):
        rc(buf, buf, ag_s.at[0], sem, CORE).wait_recv()

    def sent(buf, sem):
        rc(buf, buf, sem, ag_r.at[0], CORE).wait_send()

    own = W.at[c, yh, pa, pb]
    w_in = pltpu.make_async_copy(wgt.at[0], own, s_in.at[0])
    w_in.start()
    NH = 6
    HR = TOKD // NH
    loads = []
    for i in range(NH):
        cp = pltpu.make_async_copy(
            hid.at[0, pl.ds(i * HR, HR)], N.at[pl.ds(i * HR, HR)], s_in.at[1 + i]
        )
        cp.start()
        loads.append(cp)
    c_in = pltpu.make_async_copy(cot, CO, s_in.at[1 + NH])
    c_in.start()

    def norm(i):
        loads[i].wait()

        def body(j, carry):
            rows = pl.ds(pl.multiple_of(i * HR + j * 16, 16), 16)
            v = N[rows, :].astype(F32)
            ms = jnp.mean(v * v, axis=1, keepdims=True)
            N[rows, :] = (v * lax.rsqrt(ms + EPS) * gain[...]).astype(BF)
            return carry

        lax.fori_loop(0, HR // 16, body, 0)

    place = {"0": pb, "+": b1, "-": b3, "2": b2}
    rank = {"0": 0, "+": 1, "-": 2, "2": 3}
    half = {"m": m, "o": o}

    def shard_to(yy, a, b, s_sem, r_sem, to):
        w = W.at[c, yy, a, b]
        rc(w, w, s_sem, r_sem, to).start()

    def b_send(y, b, to, far=False):
        i = (0 if y == "m" else 2) + far
        shard_to(half[y], pa, place[b], ag_s.at[1], ag_b.at[i], to)

    def b_near(y):
        recv(W.at[c, 0, 0, 0:2], ag_b.at[0 if y == "m" else 2])

    def b_far(y):
        recv(W.at[c, 0, 0, 0], ag_b.at[1 if y == "m" else 3])

    def a_both(y, b):
        sem = ag_a.at[(0 if y == "m" else 4) + rank[b]]
        shard_to(half[y], pa, place[b], ag_s.at[2], sem, A_R)
        shard_to(half[y], pa, place[b], ag_s.at[2], sem, A_L)

    def a_relay(y, b, right):
        recv(W.at[c, 0, 0, 0:2], ag_a.at[(0 if y == "m" else 4) + rank[b]])
        sem = ag_a.at[8 if y == "m" else 9]
        if right:
            shard_to(half[y], a3, place[b], ag_s.at[2], sem, A_R)
        else:
            shard_to(half[y], a1, place[b], ag_s.at[2], sem, A_L)

    def core_send(y, a):
        w = W.at[c, half[y], a]
        rc(w, w, ag_s.at[3], ag_r.at[0], CORE).start()

    def ag0():
        w_in.wait()
        shard_to(m, pa, pb, ag_s.at[0], ag_b.at[4], Y_O)
        b_send("m", "0", B_R)
        b_send("m", "0", B_L)
        a_both("m", "0")

    def ag1():
        b_near("m")
        b_send("m", "-", B_R, True)
        recv(W.at[c, 0, 0, 0], ag_b.at[4])
        b_send("o", "0", B_R)
        b_send("o", "0", B_L)
        a_both("m", "-")
        a_both("m", "+")
        a_both("o", "0")
        a_relay("m", "0", True)

    def ag2():
        b_near("o")
        b_send("o", "+", B_L, True)
        b_far("m")
        a_both("m", "2")
        core_send("m", pa)
        a_both("o", "-")
        a_both("o", "+")

    def ag3():
        a_relay("m", "-", True)
        a_relay("m", "+", False)
        a_relay("o", "0", False)

    def ag4():
        b_far("o")
        a_both("o", "2")
        core_send("o", pa)

    def ag5():
        a_relay("m", "2", False)
        core_send("m", a3)
        core_send("m", a1)
        a_relay("o", "-", False)
        a_relay("o", "+", True)

    def ag6():
        a_relay("o", "2", True)
        core_send("o", a3)
        core_send("o", a1)

    def ag7():
        recv(W.at[c, 0, 0], ag_a.at[8])
        core_send("m", a2)
        recv(W.at[c, 0, 0], ag_a.at[9])
        core_send("o", a2)

    def ag8():
        recv(W.at[1 - c], ag_r.at[0])

    def only0(fn):
        pl.when(g == 0)(fn)

    def cols(k):
        return pl.ds(k * CW, CW)

    def turn():
        c_in.wait()

        def body(i, carry):
            at = pl.ds(pl.multiple_of(i * 128, 128), 128)
            CT[at, :] = CO[:, at].T
            return carry

        lax.fori_loop(0, KV // 128, body, 0)

    def s0(k):
        @pl.loop(0, CW // 256)
        def _(j):
            at = pl.ds(pl.multiple_of(k * CW + j * 256, 256), 256)
            for yy in range(2):
                part = jnp.dot(
                    CT[pl.ds(yy * 512, 512), :], N[:, at], preferred_element_type=F32
                ).astype(BF)
                for zz in range(4):
                    for xx in range(4):
                        for cc in range(2):
                            r = ((zz * 4 + xx) * 2 + cc) * 16
                            aa, bb = (zz, xx) if cc == 0 else (xx, zz)
                            G[cc, yy, aa, bb, :, at] = part[r : r + 16, :]

        rc(G.at[1 - c, :, :, :, :, cols(k)], PR.at[k], rs_s.at[0], rs_r.at[k, 0], CORE).start()

    def near(k, q, yy, a, to, r):
        rc(G.at[c, yy, a, :, :, cols(k)], QA.at[k, q], rs_s.at[1], rs_r.at[k, r], to).start()

    def s1(k):
        recv(PR.at[k], rs_r.at[k, 0])

        @pl.loop(0, 32)
        def _(i):
            yy, a, b = i // 16, (i // 4) % 4, i % 4
            G[c, yy, a, b, :, cols(k)] = (
                G[c, yy, a, b, :, cols(k)].astype(F32) + PR[k, yy, a, b].astype(F32)
            ).astype(BF)

        if k in LENT:
            for a, i in ((a2, 0), (a1, 1), (a3, 1), (pa, 2)):
                w = G.at[c, :, a, :, :, cols(k)]
                rc(w, w, rs_s.at[4], x_r.at[i], LEND).start()
        else:
            s1a(k)
            s1b(k)

    def s1a(k):
        near(k, 0, 0, a2, A_R, 1)
        near(k, 1, 1, a2, A_L, 1)

    def s1b(k):
        near(k, 2, 1, a1, A_R, 2)
        near(k, 3, 0, a3, A_L, 2)

    def x1(k):
        recv(G.at[c, :, 0, :, :, cols(k)], x_r.at[0])
        s1a(k)

    def x2(k):
        recv(G.at[c, :, 0:2, :, :, cols(k)], x_r.at[1])
        s1b(k)

    def x3(k):
        recv(G.at[c, :, 0, :, :, cols(k)], x_r.at[2])

    def s2(k):
        recv(QA.at[k, 0:2], rs_r.at[k, 1])
        for q, yy, a, to in ((0, 0, a1, A_R), (1, 1, a3, A_L)):

            @pl.loop(0, 4)
            def _(b, q=q, yy=yy, a=a):
                G[c, yy, a, b, :, cols(k)] = (
                    G[c, yy, a, b, :, cols(k)].astype(F32) + QA[k, q, b].astype(F32)
                ).astype(BF)

            near(k, 4 + q, yy, a, to, 2)

    def s3(k):
        recv(QA.at[k, 2:6], rs_r.at[k, 2])
        for yy, q0, q1 in ((0, 3, 4), (1, 2, 5)):

            @pl.loop(0, 4)
            def _(b, yy=yy, q0=q0, q1=q1):
                G[c, yy, pa, b, :, cols(k)] = (
                    G[c, yy, pa, b, :, cols(k)].astype(F32)
                    + (QA[k, q0, b].astype(F32) + QA[k, q1, b].astype(F32))
                ).astype(BF)

        spots = [(yh, b) for b in (b1, b3, b2)] + [(o, b) for b in (b1, b3, b2, pb)]
        for (yy, b), to in zip(spots, TEAM):
            rc(
                G.at[c, yy, pa, b, :, cols(k)], QB.at[k, yh * 4 + pb],
                rs_s.at[2], rs_r.at[k, 3], to,
            ).start()

    def s6(k):
        recv(QB.at[k, 0:7], rs_r.at[k, 3])
        tot = G[c, yh, pa, pb, :, cols(k)].astype(F32)
        for yy, b in [(yh, b1), (yh, b3), (yh, b2), (o, pb), (o, b1), (o, b3), (o, b2)]:
            tot = tot + QB[k, yy * 4 + b].astype(F32)
        FG[:, cols(k)] = tot * (D ** -0.5)

    def hand(k):
        s6(k)
        w = FG.at[:, cols(k)]
        rc(w, w, rs_s.at[3], x_r.at[3], OTHER).start()

    def take(k):
        recv(FG.at[:, cols(k)], x_r.at[3])

    def values(n):
        yy, z0 = n // 2, (n % 2) * 2
        at = pl.ds(n * VW, VW)
        for i in range(2):
            for xx in range(4):
                r = i * 128 + xx * 32
                WN[pl.ds(r, 16), :] = W[0, yy, z0 + i, xx]
                WN[pl.ds(r + 16, 16), :] = W[1, yy, xx, z0 + i]

        @pl.loop(0, 2)
        def _(h):
            rows = pl.ds(pl.multiple_of(h * 384, 128), 384)
            v = lax.dot_general(
                N[rows, :], WN[...], (((1,), (1,)), ((), ())), preferred_element_type=F32
            ) * (D ** -0.5)
            E[rows, at] = v.astype(BF)
            PO[h, 0:3, at] = jnp.mean(v.reshape(3, SEG, VW), axis=1)

        pltpu.make_async_copy(E.at[:, at], enc.at[0, :, at], s_out.at[0]).start()

    def msg1():
        p = jnp.concatenate([PO[0, 0:3, :], PO[1, 0:3, :], jnp.zeros((2, KV), F32)], axis=0)
        lo, hi = p[:, 0:512], p[:, 512:1024]
        pad = jnp.zeros((1, 64), F32)
        label = jnp.concatenate(
            [
                srow[...].astype(F32), pad, sown[...].astype(F32), pad,
                stgt[...].astype(F32), pad, jnp.zeros((1, 128), F32),
            ],
            axis=1,
        )
        line = lax.broadcasted_iota(jnp.int32, (8, 512), 0)
        lo = jnp.where(line == 6, jnp.broadcast_to(label, (8, 512)), lo)
        MS[...] = jnp.concatenate([lo, hi], axis=0).astype(BF)
        for to in CROSS:
            rc(MS, MR.at[yh, pb], ms_s.at[0], ms_r.at[0], to).start()

    def msg2():
        recv(MR, ms_r.at[0])
        rows = MR[...].reshape(8, 16, 512)
        lab = rows[:, :, 0:384].astype(F32)[:, 6:7, :]
        pick, own_, aim = lab[:, :, 0:64], lab[:, :, 128:192], lab[:, :, 256:320]
        slot = jnp.full((8, 1, 64), -1.0, F32)
        for j, i in enumerate(AIM):
            slot = jnp.where(own_ == i.astype(F32), aim + 8.0 * j, slot)
        line = lax.broadcasted_iota(jnp.int32, (16, 64), 0)
        spot = lax.broadcasted_iota(jnp.int32, (64, 64), 0).astype(F32)
        low = jnp.zeros((64, 512), F32)
        high = jnp.zeros((64, 512), F32)
        for d in range(8):
            row = jnp.broadcast_to(pick[d], (16, 64))
            lo = jnp.where(row == line.astype(F32), 1.0, 0.0).astype(BF)
            hi = jnp.where(row + 8.0 == line.astype(F32), 1.0, 0.0).astype(BF)
            to = jnp.where(jnp.broadcast_to(slot[d], (64, 64)) == spot, 1.0, 0.0).astype(BF)

            def picked(which):
                return lax.dot_general(
                    which, rows[d], (((0,), (0,)), ((), ())), preferred_element_type=F32
                ).astype(BF)

            low = low + jnp.dot(to, picked(lo), preferred_element_type=F32)
            high = high + jnp.dot(to, picked(hi), preferred_element_type=F32)
        for j in range(8):
            SP[j, 0:8, :] = low[j * 8 : j * 8 + 8, :]
            SP[j, 8:16, :] = high[j * 8 : j * 8 + 8, :]
        for j in range(1, 8):
            rc(SP.at[j], DP.at[c * 4 + pa], ms_s.at[1], ms_r.at[1], (g, AIM[j])).start()

    def deliver():
        recv(DP.at[0:7], ms_r.at[1])
        out = SP[0]
        for cc, line in ((c, (a1, a3, a2)), (1 - c, (pb, b1, b3, b2))):
            for i in line:
                out = out + DP[cc * 4 + i]
        deliv[0, :, 0:512] = out[0:POOL, :]
        deliv[0, :, 512:1024] = out[8 : 8 + POOL, :]

    def update0():
        gr = FG[...]
        scale = jnp.sqrt(jnp.mean(gr * gr, axis=1, keepdims=True) + EPS)
        t = (W[c, yh, pa, pb].astype(F32) - LEARN * gr / scale).astype(BF)
        TR[...] = t
        neww[0] = t
        rc(TR, RT, t_s, t_r, OTHER).start()

    def update1():
        recv(RT, t_r)
        neww[0] = (
            MOMENTUM * W[c, yh, pa, pb].astype(F32) + (1.0 - MOMENTUM) * RT[...].astype(F32)
        ).astype(BF)

    def finish():
        pltpu.make_async_copy(E, enc.at[0], s_out.at[0]).wait()
        sent(W.at[c, 0, 0, 0], ag_s.at[0])
        sent(W.at[c, :, 0:3, 0], ag_s.at[1])
        sent(W.at[c, :, 0:3], ag_s.at[2])
        sent(W.at[c], ag_s.at[3])
        sent(MR, ms_s.at[0])
        sent(DP.at[0:7], ms_s.at[1])

    pl.semaphore_wait(barrier, len(peers))
    ag0()
    for i in range(0, 3):
        norm(i)
    ag1()
    for i in range(3, NH):
        norm(i)

    @pl.when(g == 0)
    def _():
        turn()
        ag2()
        s0(0)
        ag3()
        s0(1)
        ag4()
        s1(0)
        s0(2)
        ag5()
        s1(1)
        s0(3)
        ag6()
        s1(2)
        ag7()
        s2(1)
        s1(3)
        ag8()
        values(0)
        s2(2)
        values(1)
        s2(3)
        s3(1)
        values(2)
        s3(2)
        values(3)
        msg1()
        s3(3)
        s6(1)
        msg2()
        s6(2)
        s6(3)
        take(0)
        update0()
        sent(PR, rs_s.at[0])
        sent(QA.at[1:NC], rs_s.at[1])
        sent(QB.at[1:NC, 0:7], rs_s.at[2])
        sent(G.at[c, :, :, :, :, cols(0)], rs_s.at[4])
        sent(TR, t_s)

    @pl.when(g == 1)
    def _():
        ag2()
        ag3()
        ag4()
        ag5()
        x1(0)
        ag6()
        x2(0)
        ag7()
        s2(0)
        x3(0)
        ag8()
        values(0)
        s3(0)
        values(1)
        values(2)
        values(3)
        msg1()
        hand(0)
        msg2()
        c_in.wait()
        sent(QA.at[0], rs_s.at[1])
        sent(QB.at[0, 0:7], rs_s.at[2])
        sent(FG.at[:, cols(0)], rs_s.at[3])

    deliver()
    pl.when(g == 1)(update1)

    finish()


def on_device(hidden, weights, gain, cotangent, send_row, send_owner, send_target):
    dma = pltpu.SemaphoreType.DMA
    vm = pltpu.VMEM
    anywhere = pl.BlockSpec(memory_space=pl.ANY)
    vmem = pl.BlockSpec(memory_space=pltpu.VMEM)
    return pl.pallas_call(
        kernel,
        out_shape=(
            jax.ShapeDtypeStruct((1, TOKD, KV), BF),
            jax.ShapeDtypeStruct((1, ROWS, D), BF),
            jax.ShapeDtypeStruct((1, POOL, KV), F32),
        ),
        in_specs=[anywhere, anywhere, vmem, anywhere, vmem, vmem, vmem],
        out_specs=(anywhere, vmem, vmem),
        scratch_shapes=[
            vm((TOKD, D), BF),
            vm((KV, TOKD), BF),
            vm((TOKD, KV), BF),
            vm((2, 2, 4, 4, ROWS, D), BF),
            vm((2, 2, 4, 4, ROWS, D), BF),
            vm((NC, 2, 4, 4, ROWS, CW), BF),
            vm((NC, 6, 4, ROWS, CW), BF),
            vm((NC, 8, ROWS, CW), BF),
            vm((ROWS, D), F32),
            vm((ROWS, D), BF),
            vm((ROWS, D), BF),
            vm((VW, D), BF),
            vm((TOKD, KV), BF),
            vm((2, 8, KV), F32),
            vm((16, 512), BF),
            vm((2, 4, 16, 512), BF),
            vm((8, 16, 512), F32),
            vm((8, 16, 512), F32),
            dma((8,)),
            dma((4,)),
            dma((5,)),
            dma((10,)),
            dma((1,)),
            dma((5,)),
            dma((NC, 4)),
            dma((4,)),
            dma,
            dma,
            dma((2,)),
            dma((2,)),
            dma((1,)),
        ],
        compiler_params=pltpu.CompilerParams(
            collective_id=0, has_side_effects=True, vmem_limit_bytes=64 * 1024 * 1024 - 131072
        ),
    )(
        hidden, weights, gain, cotangent, send_row, send_owner.reshape(1, -1), send_target
    )


def solution(mesh):
    in_specs = (
        P("grp", "fsdp", None),
        P("grp", "fsdp", None),
        P("grp", None),
        P("fsdp", None),
        P("grp", "fsdp"),
        P("grp", "fsdp", None),
        P("grp", "fsdp"),
    )
    out_specs = (P("grp", "fsdp", None), P("grp", "fsdp", None), P("grp", "fsdp", None))
    return jax.shard_map(
        on_device, mesh=mesh, in_specs=in_specs, out_specs=out_specs, check_vma=False
    )
```

```python
import jax
import jax.numpy as jnp
from jax import lax
from jax.experimental import pallas as pl
from jax.experimental.pallas import tpu as pltpu
from jax.sharding import PartitionSpec as P

MESH = pl.DeviceIdType.MESH
BF = jnp.bfloat16
F32 = jnp.float32

SEG = 128
TOKD = 768
D = 4096
KV = 1024
ROWS = 16
POOL = 6
NC = 4
CW = D // NC
NV = 4
LENT = (0,)
VW = KV // NV
EPS = 1e-06
LEARN = 0.25
MOMENTUM = 0.75


def kernel(
    hid, wgt, gain, cot, srow, sown, stgt,
    enc, neww, deliv,
    N, CT, CO, W, G, PR, QA, QB, FG, FB, WO, WN, E, PO, MS, MR, SP, DP,
    s_in, ag_s, ag_b, ag_a, ag_r, rs_s, rs_r, x_r, t_s, t_r, ms_s, ms_r, s_out,
):
    g = lax.axis_index("grp")
    f = lax.axis_index("fsdp")
    c = lax.rem(f, 2)
    x = lax.rem(lax.div(f, 2), 4)
    z = lax.rem(lax.div(f, 8), 4)
    yh = lax.div(f, 32)
    pa = z + c * (x - z)
    pb = x + c * (z - x)
    m, o = yh, 1 - yh

    def up(p, by):
        return lax.rem(p + by, 4)

    def dev(gg, yy, a, b, cc):
        zz = a + c * (b - a)
        xx = b + c * (a - b)
        return (gg, ((yy * 4 + zz) * 4 + xx) * 2 + cc)

    a1, a2, a3 = up(pa, 1), up(pa, 2), up(pa, 3)
    b1, b2, b3 = up(pb, 1), up(pb, 2), up(pb, 3)
    A_R, A_L, A_O = dev(g, yh, a1, pb, c), dev(g, yh, a3, pb, c), dev(g, yh, a2, pb, c)
    B_R, B_L = dev(g, yh, pa, b1, c), dev(g, yh, pa, b3, c)
    Y_O = dev(g, o, pa, pb, c)
    CORE = dev(g, yh, pa, pb, 1 - c)
    TEAM = [dev(g, yh, pa, b, c) for b in (b1, b3, b2)] + [
        dev(g, o, pa, b, c) for b in (b1, b3, b2, pb)
    ]
    CROSS = [dev(1 - g, yy, pa, bb, c) for yy in range(2) for bb in range(4)]
    OTHER = dev(1 - g, yh, pa, pb, c)
    LEND = dev(1 - g, yh + c * (1 - 2 * yh), pa, pb, c)

    barrier = pltpu.get_barrier_semaphore()
    flip = 1 - 2 * c
    AIM = [f] + [dev(g, yh, a, pb, c)[1] for a in (a1, a3, a2)]
    AIM = AIM + [i + flip for i in AIM]
    NEAR = [(g, dev(g, yh, pa, b, c)[1] + flip) for b in (b1, b3, b2)]
    peers = [(g, i) for i in AIM[1:]] + NEAR + TEAM + CROSS
    for peer in peers:
        pl.semaphore_signal(barrier, inc=1, device_id=peer, device_id_type=MESH)

    def rc(src, dst, ss, rs, to):
        return pltpu.make_async_remote_copy(
            src_ref=src, dst_ref=dst, send_sem=ss, recv_sem=rs, device_id=to, device_id_type=MESH
        )

    def recv(buf, sem):
        rc(buf, buf, ag_s.at[0], sem, CORE).wait_recv()

    def sent(buf, sem):
        rc(buf, buf, sem, ag_r.at[0], CORE).wait_send()

    own = W.at[c, yh, pa, pb]
    w_in = pltpu.make_async_copy(wgt.at[0], own, s_in.at[0])
    w_in.start()
    NH = 6
    HR = TOKD // NH
    loads = []
    for i in range(NH):
        cp = pltpu.make_async_copy(
            hid.at[0, pl.ds(i * HR, HR)], N.at[pl.ds(i * HR, HR)], s_in.at[1 + i]
        )
        cp.start()
        loads.append(cp)
    c_in = pltpu.make_async_copy(cot, CO, s_in.at[1 + NH])
    c_in.start()

    def norm(i):
        loads[i].wait()

        def body(j, carry):
            rows = pl.ds(pl.multiple_of(i * HR + j * 16, 16), 16)
            v = N[rows, :].astype(F32)
            ms = jnp.mean(v * v, axis=1, keepdims=True)
            N[rows, :] = (v * lax.rsqrt(ms + EPS) * gain[...]).astype(BF)
            return carry

        lax.fori_loop(0, HR // 16, body, 0)

    place = {"0": pb, "+": b1, "-": b3, "2": b2}
    rank = {"0": 0, "+": 1, "-": 2, "2": 3}
    half = {"m": m, "o": o}

    def shard_to(yy, a, b, s_sem, r_sem, to):
        w = W.at[c, yy, a, b]
        rc(w, w, s_sem, r_sem, to).start()

    def b_send(y, b, to, far=False):
        i = (0 if y == "m" else 2) + far
        shard_to(half[y], pa, place[b], ag_s.at[1], ag_b.at[i], to)

    def b_near(y):
        recv(W.at[c, 0, 0, 0:2], ag_b.at[0 if y == "m" else 2])

    def b_far(y):
        recv(W.at[c, 0, 0, 0], ag_b.at[1 if y == "m" else 3])

    def a_both(y, b):
        sem = ag_a.at[(0 if y == "m" else 4) + rank[b]]
        shard_to(half[y], pa, place[b], ag_s.at[2], sem, A_R)
        shard_to(half[y], pa, place[b], ag_s.at[2], sem, A_L)

    def a_relay(y, b, right):
        recv(W.at[c, 0, 0, 0:2], ag_a.at[(0 if y == "m" else 4) + rank[b]])
        sem = ag_a.at[10 if b == "0" else 8 if y == "m" else 9]
        if right:
            shard_to(half[y], a3, place[b], ag_s.at[2], sem, A_R)
        else:
            shard_to(half[y], a1, place[b], ag_s.at[2], sem, A_L)

    def core_send(y, a):
        w = W.at[c, half[y], a]
        rc(w, w, ag_s.at[3], ag_r.at[0], CORE).start()

    def ag0():
        w_in.wait()
        shard_to(m, pa, pb, ag_s.at[0], ag_b.at[4], Y_O)
        b_send("m", "0", B_R)
        b_send("m", "0", B_L)
        a_both("m", "0")

    def ag1():
        b_near("m")
        b_send("m", "-", B_R, True)
        recv(W.at[c, 0, 0, 0], ag_b.at[4])
        b_send("o", "0", B_R)
        b_send("o", "0", B_L)
        a_both("m", "-")
        a_both("m", "+")
        a_relay("m", "0", True)
        shard_to(m, a3, pb, ag_s.at[2], ag_a.at[4], Y_O)
        shard_to(m, a1, pb, ag_s.at[2], ag_a.at[4], Y_O)

    def ag2():
        b_near("o")
        b_send("o", "+", B_L, True)
        b_far("m")
        a_both("m", "2")
        core_send("m", pa)
        a_both("o", "-")
        a_both("o", "+")

    def ag3():
        a_relay("m", "-", True)
        a_relay("m", "+", False)
        recv(W.at[c, 0, 0, 0], ag_a.at[10])
        shard_to(m, a2, pb, ag_s.at[2], ag_a.at[11], Y_O)

    def ag4():
        b_far("o")
        a_both("o", "2")
        core_send("o", pa)

    def ag5():
        a_relay("m", "2", False)
        core_send("m", a3)
        core_send("m", a1)
        a_relay("o", "-", False)
        a_relay("o", "+", True)

    def ag6():
        a_relay("o", "2", True)
        recv(W.at[c, 0, 0, 0:2], ag_a.at[4])
        core_send("o", a3)
        core_send("o", a1)

    def ag7():
        recv(W.at[c, 0, 0, 0:3], ag_a.at[8])
        core_send("m", a2)
        recv(W.at[c, 0, 0, 0:3], ag_a.at[9])
        recv(W.at[c, 0, 0, 0], ag_a.at[11])
        core_send("o", a2)

    def ag8():
        recv(W.at[1 - c], ag_r.at[0])

    def only0(fn):
        pl.when(g == 0)(fn)

    def cols(k):
        return pl.ds(k * CW, CW)

    def turn():
        c_in.wait()

        def body(i, carry):
            at = pl.ds(pl.multiple_of(i * 128, 128), 128)
            CT[at, :] = CO[:, at].T
            return carry

        lax.fori_loop(0, KV // 128, body, 0)

    def s0(k):
        @pl.loop(0, CW // 256)
        def _(j):
            at = pl.ds(pl.multiple_of(k * CW + j * 256, 256), 256)
            for yy in range(2):
                part = jnp.dot(
                    CT[pl.ds(yy * 512, 512), :], N[:, at], preferred_element_type=F32
                ).astype(BF)
                for zz in range(4):
                    for xx in range(4):
                        for cc in range(2):
                            r = ((zz * 4 + xx) * 2 + cc) * 16
                            aa, bb = (zz, xx) if cc == 0 else (xx, zz)
                            G[cc, yy, aa, bb, :, at] = part[r : r + 16, :]

        rc(G.at[1 - c, :, :, :, :, cols(k)], PR.at[k], rs_s.at[0], rs_r.at[k, 0], CORE).start()

    def near(k, q, yy, a, to, r):
        rc(G.at[c, yy, a, :, :, cols(k)], QA.at[k, q], rs_s.at[1], rs_r.at[k, r], to).start()

    def s1(k):
        recv(PR.at[k], rs_r.at[k, 0])

        @pl.loop(0, 32)
        def _(i):
            yy, a, b = i // 16, (i // 4) % 4, i % 4
            G[c, yy, a, b, :, cols(k)] = (
                G[c, yy, a, b, :, cols(k)].astype(F32) + PR[k, yy, a, b].astype(F32)
            ).astype(BF)

        if k in LENT:
            for a, i in ((a2, 0), (a1, 1), (a3, 1), (pa, 2)):
                w = G.at[c, :, a, :, :, cols(k)]
                rc(w, w, rs_s.at[4], x_r.at[i], LEND).start()
        else:
            s1a(k)
            s1b(k)

    def s1a(k):
        near(k, 0, 0, a2, A_R, 1)
        near(k, 1, 1, a2, A_L, 1)

    def s1b(k):
        near(k, 2, 1, a1, A_R, 2)
        near(k, 3, 0, a3, A_L, 2)

    def x1(k):
        recv(G.at[c, :, 0, :, :, cols(k)], x_r.at[0])
        s1a(k)

    def x2(k):
        recv(G.at[c, :, 0:2, :, :, cols(k)], x_r.at[1])
        s1b(k)

    def x3(k):
        recv(G.at[c, :, 0, :, :, cols(k)], x_r.at[2])

    def s2(k):
        recv(QA.at[k, 0:2], rs_r.at[k, 1])
        for q, yy, a, to in ((0, 0, a1, A_R), (1, 1, a3, A_L)):

            @pl.loop(0, 4)
            def _(b, q=q, yy=yy, a=a):
                G[c, yy, a, b, :, cols(k)] = (
                    G[c, yy, a, b, :, cols(k)].astype(F32) + QA[k, q, b].astype(F32)
                ).astype(BF)

            near(k, 4 + q, yy, a, to, 2)

    def s3(k):
        recv(QA.at[k, 2:6], rs_r.at[k, 2])
        for yy, q0, q1 in ((0, 3, 4), (1, 2, 5)):

            @pl.loop(0, 4)
            def _(b, yy=yy, q0=q0, q1=q1):
                G[c, yy, pa, b, :, cols(k)] = (
                    G[c, yy, pa, b, :, cols(k)].astype(F32)
                    + (QA[k, q0, b].astype(F32) + QA[k, q1, b].astype(F32))
                ).astype(BF)

        spots = [(yh, b) for b in (b1, b3, b2)] + [(o, b) for b in (b1, b3, b2, pb)]
        for (yy, b), to in zip(spots, TEAM):
            rc(
                G.at[c, yy, pa, b, :, cols(k)], QB.at[k, yh * 4 + pb],
                rs_s.at[2], rs_r.at[k, 3], to,
            ).start()

    def s6(k):
        recv(QB.at[k, 0:7], rs_r.at[k, 3])
        tot = G[c, yh, pa, pb, :, cols(k)].astype(F32)
        for yy, b in [(yh, b1), (yh, b3), (yh, b2), (o, pb), (o, b1), (o, b3), (o, b2)]:
            tot = tot + QB[k, yy * 4 + b].astype(F32)
        FG[:, cols(k)] = tot * (D ** -0.5)

    def hand(k):
        s6(k)
        w = FG.at[:, cols(k)]
        rc(w, w, rs_s.at[3], x_r.at[3], OTHER).start()

    def take(k):
        recv(FG.at[:, cols(k)], x_r.at[3])

    def values(n):
        yy, z0 = n // 2, (n % 2) * 2
        at = pl.ds(n * VW, VW)
        for i in range(2):
            for xx in range(4):
                r = i * 128 + xx * 32
                WN[pl.ds(r, 16), :] = W[0, yy, z0 + i, xx]
                WN[pl.ds(r + 16, 16), :] = W[1, yy, xx, z0 + i]

        @pl.loop(0, 2)
        def _(h):
            rows = pl.ds(pl.multiple_of(h * 384, 128), 384)
            v = lax.dot_general(
                N[rows, :], WN[...], (((1,), (1,)), ((), ())), preferred_element_type=F32
            ) * (D ** -0.5)
            E[rows, at] = v.astype(BF)
            PO[h, 0:3, at] = jnp.mean(v.reshape(3, SEG, VW), axis=1)

        pltpu.make_async_copy(E.at[:, at], enc.at[0, :, at], s_out.at[0]).start()

    def msg1():
        p = jnp.concatenate([PO[0, 0:3, :], PO[1, 0:3, :], jnp.zeros((2, KV), F32)], axis=0)
        lo, hi = p[:, 0:512], p[:, 512:1024]
        pad = jnp.zeros((1, 64), F32)
        label = jnp.concatenate(
            [
                srow[...].astype(F32), pad, sown[...].astype(F32), pad,
                stgt[...].astype(F32), pad, jnp.zeros((1, 128), F32),
            ],
            axis=1,
        )
        line = lax.broadcasted_iota(jnp.int32, (8, 512), 0)
        lo = jnp.where(line == 6, jnp.broadcast_to(label, (8, 512)), lo)
        MS[...] = jnp.concatenate([lo, hi], axis=0).astype(BF)
        for to in CROSS:
            rc(MS, MR.at[yh, pb], ms_s.at[0], ms_r.at[0], to).start()

    def msg2():
        recv(MR, ms_r.at[0])
        rows = MR[...].reshape(8, 16, 512)
        lab = rows[:, :, 0:384].astype(F32)[:, 6:7, :]
        pick, own_, aim = lab[:, :, 0:64], lab[:, :, 128:192], lab[:, :, 256:320]
        slot = jnp.full((8, 1, 64), -1.0, F32)
        for j, i in enumerate(AIM):
            slot = jnp.where(own_ == i.astype(F32), aim + 8.0 * j, slot)
        slots = jnp.concatenate([slot[d] for d in range(8)], axis=1)
        picks = jnp.concatenate([pick[d] + 16.0 * d for d in range(8)], axis=1)
        spot = lax.broadcasted_iota(jnp.int32, (64, 512), 0).astype(F32)
        line = lax.broadcasted_iota(jnp.int32, (128, 512), 0).astype(F32)
        to = jnp.where(slots == spot, 1.0, 0.0).astype(BF)

        def summed(by):
            which = jnp.where(picks + by == line, 1.0, 0.0).astype(BF)
            table = lax.dot_general(
                to, which, (((1,), (1,)), ((), ())), preferred_element_type=F32
            )
            return jnp.dot(
                table.astype(BF), rows.reshape(128, 512), preferred_element_type=F32
            )

        low, high = summed(0.0), summed(8.0)
        for j in range(8):
            SP[j, 0:8, :] = low[j * 8 : j * 8 + 8, :]
            SP[j, 8:16, :] = high[j * 8 : j * 8 + 8, :]
        for j in range(1, 8):
            rc(SP.at[j], DP.at[c * 4 + pa], ms_s.at[1], ms_r.at[1], (g, AIM[j])).start()

    def deliver():
        recv(DP.at[0:7], ms_r.at[1])
        out = SP[0]
        for cc, line in ((c, (a1, a3, a2)), (1 - c, (pb, b1, b3, b2))):
            for i in line:
                out = out + DP[cc * 4 + i]
        for t in range(POOL):
            deliv[t, :, 0:512] = out[t : t + 1, :]
            deliv[t, :, 512:1024] = out[8 + t : 9 + t, :]

    def trained(w, gr):
        scale = jnp.sqrt(jnp.mean(gr * gr, axis=1, keepdims=True) + EPS)
        return (w.astype(F32) - LEARN * gr / scale).astype(BF)

    def give():
        w = W.at[c, yh, pa, pb]
        rc(w, WO, t_s.at[0], t_r.at[0], OTHER).start()

    def tell(k):
        FB[:, cols(k)] = FG[:, cols(k)].astype(BF)
        w = FB.at[:, cols(k)]
        rc(w, w, t_s.at[1], t_r.at[1], OTHER).start()

    def update0():
        neww[0] = trained(W[c, yh, pa, pb], FG[...])

    def update1():
        recv(WO, t_r.at[0])
        recv(FB.at[:, pl.ds(CW, D - CW)], t_r.at[1])
        FG[:, pl.ds(CW, D - CW)] = FB[:, pl.ds(CW, D - CW)].astype(F32)
        neww[0] = (
            MOMENTUM * W[c, yh, pa, pb].astype(F32)
            + (1.0 - MOMENTUM) * trained(WO[...], FG[...]).astype(F32)
        ).astype(BF)

    def finish():
        pltpu.make_async_copy(E, enc.at[0], s_out.at[0]).wait()
        sent(W.at[c, 0, 0, 0], ag_s.at[0])
        sent(W.at[c, :, 0:3, 0], ag_s.at[1])
        sent(W.at[c, :, 0:3], ag_s.at[2])
        sent(W.at[c], ag_s.at[3])
        sent(MR, ms_s.at[0])
        sent(DP.at[0:7], ms_s.at[1])

    pl.semaphore_wait(barrier, len(peers))
    ag0()
    for i in range(0, 3):
        norm(i)
    ag1()
    for i in range(3, NH):
        norm(i)

    @pl.when(g == 0)
    def _():
        turn()
        give()
        s0(0)
        ag2()
        s0(1)
        ag3()
        s1(0)
        ag4()
        s0(2)
        s1(1)
        ag5()
        s0(3)
        ag6()
        s1(2)
        ag7()
        s2(1)
        s1(3)
        ag8()
        values(0)
        s2(2)
        values(1)
        s2(3)
        s3(1)
        values(2)
        s3(2)
        values(3)
        msg1()
        s3(3)
        s6(1)
        tell(1)
        msg2()
        s6(2)
        tell(2)
        s6(3)
        tell(3)
        take(0)
        update0()
        sent(PR, rs_s.at[0])
        sent(QA.at[1:NC], rs_s.at[1])
        sent(QB.at[1:NC, 0:7], rs_s.at[2])
        sent(G.at[c, :, :, :, :, cols(0)], rs_s.at[4])
        sent(WO, t_s.at[0])
        sent(FB.at[:, pl.ds(CW, D - CW)], t_s.at[1])

    @pl.when(g == 1)
    def _():
        ag2()
        ag3()
        ag4()
        ag5()
        ag6()
        ag7()
        x1(0)
        ag8()
        values(0)
        x2(0)
        values(1)
        s2(0)
        x3(0)
        values(2)
        values(3)
        msg1()
        s3(0)
        hand(0)
        msg2()
        c_in.wait()
        sent(QA.at[0], rs_s.at[1])
        sent(QB.at[0, 0:7], rs_s.at[2])
        sent(FG.at[:, cols(0)], rs_s.at[3])

    deliver()
    pl.when(g == 1)(update1)

    finish()


NP = 6


def place_outputs(enc, neww, deliv, enc_out, neww_out, deliv_out, e, w, d, i_sem, o_sem):
    step = TOKD // NP
    parts = [(enc, e, enc_out, pl.ds(i * step, step)) for i in range(NP)]
    ins, outs = [], []
    for i, (src, mid, dst, at) in enumerate(parts):
        ins.append(pltpu.make_async_copy(src.at[:, at], mid.at[:, at], i_sem.at[i]))
        outs.append(pltpu.make_async_copy(mid.at[:, at], dst.at[:, at], o_sem.at[i]))
    for i, (src, mid, dst) in enumerate(((neww, w, neww_out), (deliv, d, deliv_out))):
        ins.append(pltpu.make_async_copy(src, mid, i_sem.at[NP + i]))
        outs.append(pltpu.make_async_copy(mid, dst, o_sem.at[NP + i]))
    for cp in ins:
        cp.start()
    for a, b in zip(ins, outs):
        a.wait()
        b.start()
    for cp in outs:
        cp.wait()


def on_device(hidden, weights, gain, cotangent, send_row, send_owner, send_target):
    dma = pltpu.SemaphoreType.DMA
    vm = pltpu.VMEM
    anywhere = pl.BlockSpec(memory_space=pl.ANY)
    vmem = pl.BlockSpec(memory_space=pltpu.VMEM)
    made = pl.pallas_call(
        kernel,
        out_shape=(
            jax.ShapeDtypeStruct((1, TOKD, KV), BF),
            jax.ShapeDtypeStruct((1, ROWS, D), BF),
            jax.ShapeDtypeStruct((POOL, 1, KV), F32),
        ),
        in_specs=[anywhere, anywhere, vmem, anywhere, vmem, vmem, vmem],
        out_specs=(anywhere, vmem, vmem),
        scratch_shapes=[
            vm((TOKD, D), BF),
            vm((KV, TOKD), BF),
            vm((TOKD, KV), BF),
            vm((2, 2, 4, 4, ROWS, D), BF),
            vm((2, 2, 4, 4, ROWS, D), BF),
            vm((NC, 2, 4, 4, ROWS, CW), BF),
            vm((NC, 6, 4, ROWS, CW), BF),
            vm((NC, 8, ROWS, CW), BF),
            vm((ROWS, D), F32),
            vm((ROWS, D), BF),
            vm((ROWS, D), BF),
            vm((VW, D), BF),
            vm((TOKD, KV), BF),
            vm((2, 8, KV), F32),
            vm((16, 512), BF),
            vm((2, 4, 16, 512), BF),
            vm((8, 16, 512), F32),
            vm((8, 16, 512), F32),
            dma((8,)),
            dma((4,)),
            dma((5,)),
            dma((12,)),
            dma((1,)),
            dma((5,)),
            dma((NC, 4)),
            dma((4,)),
            dma((2,)),
            dma((2,)),
            dma((2,)),
            dma((2,)),
            dma((1,)),
        ],
        compiler_params=pltpu.CompilerParams(
            collective_id=0, has_side_effects=True, vmem_limit_bytes=64 * 1024 * 1024 - 131072
        ),
    )(
        hidden, weights, gain, cotangent, send_row, send_owner.reshape(1, -1), send_target
    )
    enc, neww, deliv = pl.pallas_call(
        place_outputs,
        out_shape=tuple(jax.ShapeDtypeStruct(a.shape, a.dtype) for a in made),
        in_specs=[anywhere] * 3,
        out_specs=(anywhere,) * 3,
        scratch_shapes=[
            vm((1, TOKD, KV), BF),
            vm((1, ROWS, D), BF),
            vm((POOL, 1, KV), F32),
            dma((NP + 2,)),
            dma((NP + 2,)),
        ],
        compiler_params=pltpu.CompilerParams(vmem_limit_bytes=64 * 1024 * 1024 - 131072),
    )(*made)
    return enc, neww, jnp.swapaxes(deliv, 0, 1)


def solution(mesh):
    in_specs = (
        P("grp", "fsdp", None),
        P("grp", "fsdp", None),
        P("grp", None),
        P("fsdp", None),
        P("grp", "fsdp"),
        P("grp", "fsdp", None),
        P("grp", "fsdp"),
    )
    out_specs = (P("grp", "fsdp", None), P("grp", "fsdp", None), P("grp", "fsdp", None))
    return jax.shard_map(
        on_device, mesh=mesh, in_specs=in_specs, out_specs=out_specs, check_vma=False
    )
```

```python
import jax
import jax.numpy as jnp
from jax import lax
from jax.experimental import pallas as pl
from jax.experimental.pallas import tpu as pltpu
from jax.sharding import PartitionSpec as P

MESH = pl.DeviceIdType.MESH
BF = jnp.bfloat16
F32 = jnp.float32

SEG = 128
TOKD = 768
D = 4096
KV = 1024
ROWS = 16
POOL = 6
NC = 4
CW = D // NC
NV = 4
LENT = (0,)
VW = KV // NV
EPS = 1e-06
LEARN = 0.25
MOMENTUM = 0.75


def kernel(
    hid, wgt, gain, cot, srow, sown, stgt,
    enc, neww, deliv,
    N, CT, CO, W, G, PR, QA, QB, FG, FB, WO, WN, E, PO, MS, MR, SP, DP,
    s_in, ag_s, ag_b, ag_a, ag_r, rs_s, rs_r, x_r, t_s, t_r, ms_s, ms_r, s_out,
):
    g = lax.axis_index("grp")
    f = lax.axis_index("fsdp")
    c = lax.rem(f, 2)
    x = lax.rem(lax.div(f, 2), 4)
    z = lax.rem(lax.div(f, 8), 4)
    yh = lax.div(f, 32)
    pa = z + c * (x - z)
    pb = x + c * (z - x)
    m, o = yh, 1 - yh

    def up(p, by):
        return lax.rem(p + by, 4)

    def dev(gg, yy, a, b, cc):
        zz = a + c * (b - a)
        xx = b + c * (a - b)
        return (gg, ((yy * 4 + zz) * 4 + xx) * 2 + cc)

    a1, a2, a3 = up(pa, 1), up(pa, 2), up(pa, 3)
    b1, b2, b3 = up(pb, 1), up(pb, 2), up(pb, 3)
    A_R, A_L, A_O = dev(g, yh, a1, pb, c), dev(g, yh, a3, pb, c), dev(g, yh, a2, pb, c)
    B_R, B_L = dev(g, yh, pa, b1, c), dev(g, yh, pa, b3, c)
    Y_O = dev(g, o, pa, pb, c)
    CORE = dev(g, yh, pa, pb, 1 - c)
    TEAM = [dev(g, yh, pa, b, c) for b in (b1, b3, b2)] + [
        dev(g, o, pa, b, c) for b in (b1, b3, b2, pb)
    ]
    CROSS = [dev(1 - g, yy, pa, bb, c) for yy in range(2) for bb in range(4)]
    OTHER = dev(1 - g, yh, pa, pb, c)
    LEND = dev(1 - g, yh + c * (1 - 2 * yh), pa, pb, c)

    barrier = pltpu.get_barrier_semaphore()
    flip = 1 - 2 * c
    AIM = [f] + [dev(g, yh, a, pb, c)[1] for a in (a1, a3, a2)]
    AIM = AIM + [i + flip for i in AIM]
    NEAR = [(g, dev(g, yh, pa, b, c)[1] + flip) for b in (b1, b3, b2)]
    peers = [(g, i) for i in AIM[1:]] + NEAR + TEAM + CROSS
    for peer in peers:
        pl.semaphore_signal(barrier, inc=1, device_id=peer, device_id_type=MESH)

    def rc(src, dst, ss, rs, to):
        return pltpu.make_async_remote_copy(
            src_ref=src, dst_ref=dst, send_sem=ss, recv_sem=rs, device_id=to, device_id_type=MESH
        )

    def recv(buf, sem):
        rc(buf, buf, ag_s.at[0], sem, CORE).wait_recv()

    def sent(buf, sem):
        rc(buf, buf, sem, ag_r.at[0], CORE).wait_send()

    own = W.at[c, yh, pa, pb]
    w_in = pltpu.make_async_copy(wgt.at[0], own, s_in.at[0])
    w_in.start()
    NH = 6
    HR = TOKD // NH
    loads = []
    for i in range(NH):
        cp = pltpu.make_async_copy(
            hid.at[0, pl.ds(i * HR, HR)], N.at[pl.ds(i * HR, HR)], s_in.at[1 + i]
        )
        cp.start()
        loads.append(cp)
    c_in = pltpu.make_async_copy(cot, CO, s_in.at[1 + NH])
    c_in.start()

    def norm(i):
        loads[i].wait()

        def body(j, carry):
            rows = pl.ds(pl.multiple_of(i * HR + j * 16, 16), 16)
            v = N[rows, :].astype(F32)
            ms = jnp.mean(v * v, axis=1, keepdims=True)
            N[rows, :] = (v * lax.rsqrt(ms + EPS) * gain[...]).astype(BF)
            return carry

        lax.fori_loop(0, HR // 16, body, 0)

    place = {"0": pb, "+": b1, "-": b3, "2": b2}
    rank = {"0": 0, "+": 1, "-": 2, "2": 3}
    half = {"m": m, "o": o}

    def shard_to(yy, a, b, s_sem, r_sem, to):
        w = W.at[c, yy, a, b]
        rc(w, w, s_sem, r_sem, to).start()

    def b_send(y, b, to, far=False):
        i = (0 if y == "m" else 2) + far
        shard_to(half[y], pa, place[b], ag_s.at[1], ag_b.at[i], to)

    def b_near(y):
        recv(W.at[c, 0, 0, 0:2], ag_b.at[0 if y == "m" else 2])

    def b_far(y):
        recv(W.at[c, 0, 0, 0], ag_b.at[1 if y == "m" else 3])

    def a_both(y, b):
        sem = ag_a.at[(0 if y == "m" else 4) + rank[b]]
        shard_to(half[y], pa, place[b], ag_s.at[2], sem, A_R)
        shard_to(half[y], pa, place[b], ag_s.at[2], sem, A_L)

    def a_relay(y, b, right):
        recv(W.at[c, 0, 0, 0:2], ag_a.at[(0 if y == "m" else 4) + rank[b]])
        sem = ag_a.at[10 if b == "0" else 8 if y == "m" else 9]
        if right:
            shard_to(half[y], a3, place[b], ag_s.at[2], sem, A_R)
        else:
            shard_to(half[y], a1, place[b], ag_s.at[2], sem, A_L)

    def core_send(y, a):
        w = W.at[c, half[y], a]
        rc(w, w, ag_s.at[3], ag_r.at[0 if y == "m" else 1], CORE).start()

    def ag0():
        w_in.wait()
        shard_to(m, pa, pb, ag_s.at[0], ag_b.at[4], Y_O)
        b_send("m", "0", B_R)
        b_send("m", "0", B_L)
        a_both("m", "0")

    def ag1():
        b_near("m")
        b_send("m", "-", B_R, True)
        recv(W.at[c, 0, 0, 0], ag_b.at[4])
        b_send("o", "0", B_R)
        b_send("o", "0", B_L)
        a_both("m", "-")
        a_both("m", "+")
        a_relay("m", "0", True)
        shard_to(m, a3, pb, ag_s.at[2], ag_a.at[4], Y_O)
        shard_to(m, a1, pb, ag_s.at[2], ag_a.at[4], Y_O)

    def ag2():
        b_near("o")
        b_send("o", "+", B_L, True)
        b_far("m")
        a_both("m", "2")
        core_send("m", pa)
        a_both("o", "-")
        a_both("o", "+")

    def ag3():
        a_relay("m", "-", True)
        a_relay("m", "+", False)
        recv(W.at[c, 0, 0, 0], ag_a.at[10])
        shard_to(m, a2, pb, ag_s.at[2], ag_a.at[11], Y_O)

    def ag4():
        b_far("o")
        a_both("o", "2")
        core_send("o", pa)

    def ag5():
        a_relay("m", "2", False)
        core_send("m", a3)
        core_send("m", a1)
        a_relay("o", "-", False)
        a_relay("o", "+", True)

    def ag6():
        a_relay("o", "2", True)
        recv(W.at[c, 0, 0, 0:2], ag_a.at[4])
        core_send("o", a3)
        core_send("o", a1)

    def ag7():
        recv(W.at[c, 0, 0, 0:3], ag_a.at[8])
        core_send("m", a2)

    def ag8():
        recv(W.at[c, 0, 0, 0:3], ag_a.at[9])
        recv(W.at[c, 0, 0, 0], ag_a.at[11])
        core_send("o", a2)

    def ag9():
        recv(W.at[1 - c, 0], ag_r.at[0])

    def ag10():
        recv(W.at[1 - c, 0], ag_r.at[1])

    def only0(fn):
        pl.when(g == 0)(fn)

    def cols(k):
        return pl.ds(k * CW, CW)

    def turn():
        c_in.wait()

        def body(i, carry):
            at = pl.ds(pl.multiple_of(i * 128, 128), 128)
            CT[at, :] = CO[:, at].T
            return carry

        lax.fori_loop(0, KV // 128, body, 0)

    def s0(k):
        @pl.loop(0, CW // 256)
        def _(j):
            at = pl.ds(pl.multiple_of(k * CW + j * 256, 256), 256)
            for yy in range(2):
                part = jnp.dot(
                    CT[pl.ds(yy * 512, 512), :], N[:, at], preferred_element_type=F32
                ).astype(BF)
                for zz in range(4):
                    for xx in range(4):
                        for cc in range(2):
                            r = ((zz * 4 + xx) * 2 + cc) * 16
                            aa, bb = (zz, xx) if cc == 0 else (xx, zz)
                            G[cc, yy, aa, bb, :, at] = part[r : r + 16, :]

        rc(G.at[1 - c, :, :, :, :, cols(k)], PR.at[k], rs_s.at[0], rs_r.at[k, 0], CORE).start()

    def near(k, q, yy, a, to, r):
        rc(G.at[c, yy, a, :, :, cols(k)], QA.at[k, q], rs_s.at[1], rs_r.at[k, r], to).start()

    def s1(k):
        recv(PR.at[k], rs_r.at[k, 0])

        @pl.loop(0, 32)
        def _(i):
            yy, a, b = i // 16, (i // 4) % 4, i % 4
            G[c, yy, a, b, :, cols(k)] = (
                G[c, yy, a, b, :, cols(k)].astype(F32) + PR[k, yy, a, b].astype(F32)
            ).astype(BF)

        if k in LENT:
            for a, i in ((a2, 0), (a1, 1), (a3, 1), (pa, 2)):
                w = G.at[c, :, a, :, :, cols(k)]
                rc(w, w, rs_s.at[4], x_r.at[i], LEND).start()
        else:
            s1a(k)
            s1b(k)

    def s1a(k):
        near(k, 0, 0, a2, A_R, 1)
        near(k, 1, 1, a2, A_L, 1)

    def s1b(k):
        near(k, 2, 1, a1, A_R, 2)
        near(k, 3, 0, a3, A_L, 2)

    def x1(k):
        recv(G.at[c, :, 0, :, :, cols(k)], x_r.at[0])
        s1a(k)

    def x2(k):
        recv(G.at[c, :, 0:2, :, :, cols(k)], x_r.at[1])
        s1b(k)

    def x3(k):
        recv(G.at[c, :, 0, :, :, cols(k)], x_r.at[2])

    def s2(k):
        recv(QA.at[k, 0:2], rs_r.at[k, 1])
        for q, yy, a, to in ((0, 0, a1, A_R), (1, 1, a3, A_L)):

            @pl.loop(0, 4)
            def _(b, q=q, yy=yy, a=a):
                G[c, yy, a, b, :, cols(k)] = (
                    G[c, yy, a, b, :, cols(k)].astype(F32) + QA[k, q, b].astype(F32)
                ).astype(BF)

            near(k, 4 + q, yy, a, to, 2)

    def s3(k):
        recv(QA.at[k, 2:6], rs_r.at[k, 2])
        for yy, q0, q1 in ((0, 3, 4), (1, 2, 5)):

            @pl.loop(0, 4)
            def _(b, yy=yy, q0=q0, q1=q1):
                G[c, yy, pa, b, :, cols(k)] = (
                    G[c, yy, pa, b, :, cols(k)].astype(F32)
                    + (QA[k, q0, b].astype(F32) + QA[k, q1, b].astype(F32))
                ).astype(BF)

        spots = [(yh, b) for b in (b1, b3, b2)] + [(o, b) for b in (b1, b3, b2, pb)]
        for (yy, b), to in zip(spots, TEAM):
            rc(
                G.at[c, yy, pa, b, :, cols(k)], QB.at[k, yh * 4 + pb],
                rs_s.at[2], rs_r.at[k, 3], to,
            ).start()

    def s6(k):
        recv(QB.at[k, 0:7], rs_r.at[k, 3])
        tot = G[c, yh, pa, pb, :, cols(k)].astype(F32)
        for yy, b in [(yh, b1), (yh, b3), (yh, b2), (o, pb), (o, b1), (o, b3), (o, b2)]:
            tot = tot + QB[k, yy * 4 + b].astype(F32)
        FG[:, cols(k)] = tot * (D ** -0.5)

    def hand(k):
        s6(k)
        w = FG.at[:, cols(k)]
        rc(w, w, rs_s.at[3], x_r.at[3], OTHER).start()

    def take(k):
        recv(FG.at[:, cols(k)], x_r.at[3])

    def values(n):
        yy, z0 = (m, o)[n // 2], (n % 2) * 2
        at = pl.ds(pl.multiple_of((yy * 2 + n % 2) * VW, VW), VW)
        for i in range(2):
            for xx in range(4):
                r = i * 128 + xx * 32
                WN[pl.ds(r, 16), :] = W[0, yy, z0 + i, xx]
                WN[pl.ds(r + 16, 16), :] = W[1, yy, xx, z0 + i]

        @pl.loop(0, 2)
        def _(h):
            rows = pl.ds(pl.multiple_of(h * 384, 128), 384)
            v = lax.dot_general(
                N[rows, :], WN[...], (((1,), (1,)), ((), ())), preferred_element_type=F32
            ) * (D ** -0.5)
            E[rows, at] = v.astype(BF)
            PO[h, 0:3, at] = jnp.mean(v.reshape(3, SEG, VW), axis=1)

        pltpu.make_async_copy(E.at[:, at], enc.at[0, :, at], s_out.at[0]).start()

    def msg1():
        p = jnp.concatenate([PO[0, 0:3, :], PO[1, 0:3, :], jnp.zeros((2, KV), F32)], axis=0)
        lo, hi = p[:, 0:512], p[:, 512:1024]
        pad = jnp.zeros((1, 64), F32)
        label = jnp.concatenate(
            [
                srow[...].astype(F32), pad, sown[...].astype(F32), pad,
                stgt[...].astype(F32), pad, jnp.zeros((1, 128), F32),
            ],
            axis=1,
        )
        line = lax.broadcasted_iota(jnp.int32, (8, 512), 0)
        lo = jnp.where(line == 6, jnp.broadcast_to(label, (8, 512)), lo)
        MS[...] = jnp.concatenate([lo, hi], axis=0).astype(BF)
        for to in CROSS:
            rc(MS, MR.at[yh, pb], ms_s.at[0], ms_r.at[0], to).start()

    def msg2():
        recv(MR, ms_r.at[0])
        rows = MR[...].reshape(8, 16, 512)
        lab = rows[:, :, 0:384].astype(F32)[:, 6:7, :]
        pick, own_, aim = lab[:, :, 0:64], lab[:, :, 128:192], lab[:, :, 256:320]
        slot = jnp.full((8, 1, 64), -1.0, F32)
        for j, i in enumerate(AIM):
            slot = jnp.where(own_ == i.astype(F32), aim + 8.0 * j, slot)
        slots = jnp.concatenate([slot[d] for d in range(8)], axis=1)
        picks = jnp.concatenate([pick[d] + 16.0 * d for d in range(8)], axis=1)
        spot = lax.broadcasted_iota(jnp.int32, (64, 512), 0).astype(F32)
        line = lax.broadcasted_iota(jnp.int32, (128, 512), 0).astype(F32)
        to = jnp.where(slots == spot, 1.0, 0.0).astype(BF)

        def summed(by):
            which = jnp.where(picks + by == line, 1.0, 0.0).astype(BF)
            table = lax.dot_general(
                to, which, (((1,), (1,)), ((), ())), preferred_element_type=F32
            )
            return jnp.dot(
                table.astype(BF), rows.reshape(128, 512), preferred_element_type=F32
            )

        low, high = summed(0.0), summed(8.0)
        for j in range(8):
            SP[j, 0:8, :] = low[j * 8 : j * 8 + 8, :]
            SP[j, 8:16, :] = high[j * 8 : j * 8 + 8, :]
        for j in range(1, 8):
            rc(SP.at[j], DP.at[c * 4 + pa], ms_s.at[1], ms_r.at[1], (g, AIM[j])).start()

    def deliver():
        recv(DP.at[0:7], ms_r.at[1])
        out = SP[0]
        for cc, line in ((c, (a1, a3, a2)), (1 - c, (pb, b1, b3, b2))):
            for i in line:
                out = out + DP[cc * 4 + i]
        for t in range(POOL):
            deliv[t, :, 0:512] = out[t : t + 1, :]
            deliv[t, :, 512:1024] = out[8 + t : 9 + t, :]

    def trained(w, gr):
        scale = jnp.sqrt(jnp.mean(gr * gr, axis=1, keepdims=True) + EPS)
        return (w.astype(F32) - LEARN * gr / scale).astype(BF)

    def give():
        w = W.at[c, yh, pa, pb]
        rc(w, WO, t_s.at[0], t_r.at[0], OTHER).start()

    def tell(k):
        FB[:, cols(k)] = FG[:, cols(k)].astype(BF)
        w = FB.at[:, cols(k)]
        rc(w, w, t_s.at[1], t_r.at[1], OTHER).start()

    def update0():
        neww[0] = trained(W[c, yh, pa, pb], FG[...])

    def update1():
        recv(WO, t_r.at[0])
        recv(FB.at[:, pl.ds(CW, D - CW)], t_r.at[1])
        FG[:, pl.ds(CW, D - CW)] = FB[:, pl.ds(CW, D - CW)].astype(F32)
        neww[0] = (
            MOMENTUM * W[c, yh, pa, pb].astype(F32)
            + (1.0 - MOMENTUM) * trained(WO[...], FG[...]).astype(F32)
        ).astype(BF)

    def finish():
        pltpu.make_async_copy(E, enc.at[0], s_out.at[0]).wait()
        sent(W.at[c, 0, 0, 0], ag_s.at[0])
        sent(W.at[c, :, 0:3, 0], ag_s.at[1])
        sent(W.at[c, :, 0:3], ag_s.at[2])
        sent(W.at[c], ag_s.at[3])
        sent(MR, ms_s.at[0])
        sent(DP.at[0:7], ms_s.at[1])

    pl.semaphore_wait(barrier, len(peers))
    ag0()
    for i in range(0, 4):
        norm(i)
    ag1()
    for i in range(4, NH):
        norm(i)

    @pl.when(g == 0)
    def _():
        turn()
        give()
        s0(0)
        ag2()
        s0(1)
        ag3()
        s1(0)
        ag4()
        s0(2)
        s1(1)
        ag5()
        s0(3)
        ag6()
        s1(2)
        ag7()
        s2(1)
        s1(3)
        ag9()
        values(0)
        ag8()
        s2(2)
        values(1)
        ag10()
        s3(1)
        s2(3)
        values(2)
        values(3)
        msg1()
        s3(2)
        s3(3)
        s6(1)
        tell(1)
        msg2()
        s6(2)
        tell(2)
        s6(3)
        tell(3)
        take(0)
        update0()
        sent(PR, rs_s.at[0])
        sent(QA.at[1:NC], rs_s.at[1])
        sent(QB.at[1:NC, 0:7], rs_s.at[2])
        sent(G.at[c, :, :, :, :, cols(0)], rs_s.at[4])
        sent(WO, t_s.at[0])
        sent(FB.at[:, pl.ds(CW, D - CW)], t_s.at[1])

    @pl.when(g == 1)
    def _():
        ag2()
        ag3()
        ag4()
        ag5()
        ag6()
        x1(0)
        ag7()
        ag9()
        values(0)
        ag8()
        x2(0)
        values(1)
        s2(0)
        x3(0)
        ag10()
        values(2)
        values(3)
        msg1()
        s3(0)
        hand(0)
        msg2()
        c_in.wait()
        sent(QA.at[0], rs_s.at[1])
        sent(QB.at[0, 0:7], rs_s.at[2])
        sent(FG.at[:, cols(0)], rs_s.at[3])

    deliver()
    pl.when(g == 1)(update1)

    finish()


NP = 6


def place_outputs(enc, neww, deliv, enc_out, neww_out, deliv_out, e, w, d, i_sem, o_sem):
    step = TOKD // NP
    parts = [(enc, e, enc_out, pl.ds(i * step, step)) for i in range(NP)]
    ins, outs = [], []
    for i, (src, mid, dst, at) in enumerate(parts):
        ins.append(pltpu.make_async_copy(src.at[:, at], mid.at[:, at], i_sem.at[i]))
        outs.append(pltpu.make_async_copy(mid.at[:, at], dst.at[:, at], o_sem.at[i]))
    for i, (src, mid, dst) in enumerate(((neww, w, neww_out), (deliv, d, deliv_out))):
        ins.append(pltpu.make_async_copy(src, mid, i_sem.at[NP + i]))
        outs.append(pltpu.make_async_copy(mid, dst, o_sem.at[NP + i]))
    for cp in ins:
        cp.start()
    for a, b in zip(ins, outs):
        a.wait()
        b.start()
    for cp in outs:
        cp.wait()


def on_device(hidden, weights, gain, cotangent, send_row, send_owner, send_target):
    dma = pltpu.SemaphoreType.DMA
    vm = pltpu.VMEM
    anywhere = pl.BlockSpec(memory_space=pl.ANY)
    vmem = pl.BlockSpec(memory_space=pltpu.VMEM)
    made = pl.pallas_call(
        kernel,
        out_shape=(
            jax.ShapeDtypeStruct((1, TOKD, KV), BF),
            jax.ShapeDtypeStruct((1, ROWS, D), BF),
            jax.ShapeDtypeStruct((POOL, 1, KV), F32),
        ),
        in_specs=[anywhere, anywhere, vmem, anywhere, vmem, vmem, vmem],
        out_specs=(anywhere, vmem, vmem),
        scratch_shapes=[
            vm((TOKD, D), BF),
            vm((KV, TOKD), BF),
            vm((TOKD, KV), BF),
            vm((2, 2, 4, 4, ROWS, D), BF),
            vm((2, 2, 4, 4, ROWS, D), BF),
            vm((NC, 2, 4, 4, ROWS, CW), BF),
            vm((NC, 6, 4, ROWS, CW), BF),
            vm((NC, 8, ROWS, CW), BF),
            vm((ROWS, D), F32),
            vm((ROWS, D), BF),
            vm((ROWS, D), BF),
            vm((VW, D), BF),
            vm((TOKD, KV), BF),
            vm((2, 8, KV), F32),
            vm((16, 512), BF),
            vm((2, 4, 16, 512), BF),
            vm((8, 16, 512), F32),
            vm((8, 16, 512), F32),
            dma((8,)),
            dma((4,)),
            dma((5,)),
            dma((12,)),
            dma((2,)),
            dma((5,)),
            dma((NC, 4)),
            dma((4,)),
            dma((2,)),
            dma((2,)),
            dma((2,)),
            dma((2,)),
            dma((1,)),
        ],
        compiler_params=pltpu.CompilerParams(
            collective_id=0, has_side_effects=True, vmem_limit_bytes=64 * 1024 * 1024 - 131072
        ),
    )(
        hidden, weights, gain, cotangent, send_row, send_owner.reshape(1, -1), send_target
    )
    enc, neww, deliv = pl.pallas_call(
        place_outputs,
        out_shape=tuple(jax.ShapeDtypeStruct(a.shape, a.dtype) for a in made),
        in_specs=[anywhere] * 3,
        out_specs=(anywhere,) * 3,
        scratch_shapes=[
            vm((1, TOKD, KV), BF),
            vm((1, ROWS, D), BF),
            vm((POOL, 1, KV), F32),
            dma((NP + 2,)),
            dma((NP + 2,)),
        ],
        compiler_params=pltpu.CompilerParams(vmem_limit_bytes=64 * 1024 * 1024 - 131072),
    )(*made)
    return enc, neww, jnp.swapaxes(deliv, 0, 1)


def solution(mesh):
    in_specs = (
        P("grp", "fsdp", None),
        P("grp", "fsdp", None),
        P("grp", None),
        P("fsdp", None),
        P("grp", "fsdp"),
        P("grp", "fsdp", None),
        P("grp", "fsdp"),
    )
    out_specs = (P("grp", "fsdp", None), P("grp", "fsdp", None), P("grp", "fsdp", None))
    return jax.shard_map(
        on_device, mesh=mesh, in_specs=in_specs, out_specs=out_specs, check_vma=False
    )
```
